128 devices in a mesh: req: 32 (over y, x, core), kv: 4 (over z).
Axes of the slice: x: 4, y: 4, z: 4, core: 2. Of those that a mesh axis runs over, the one named last changes fastest.
Arguments:
- tokens: bfloat16 [4096, 2048], P('req'), may hold values from -6 to 6
- lengths: int32 [4096], replicated, may hold values from 1 to 1024, as said below
- page_table: int32 [4096, 16], P('req'), may hold values from 0 to 367, as said below
- key_cache: bfloat16 [11776, 4, 64, 128], P('req', 'kv'), may hold values from -320 to 320
- value_page_cache: bfloat16 [11776, 4, 64, 128], P('req', 'kv'), may hold values from -6 to 6
- mig_slot: int32 [32, 2], replicated, may hold values from 0 to 127, as said below
- attn_gain: float32 [2048], replicated, may hold values from 0.1 to 1.9
- w_query: bfloat16 [2048, 4096], P(None, 'kv'), may hold values from -0.125 to 0.125
- key_weight: bfloat16 [2048, 512], P(None, 'kv'), may hold values from -0.125 to 0.125
- value_weight: bfloat16 [2048, 512], P(None, 'kv'), may hold values from -0.125 to 0.125
- w_out: bfloat16 [4096, 2048], P('kv'), may hold values from -0.09375 to 0.09375
- moe_gain: float32 [2048], replicated, may hold values from 0.1 to 1.9
- routes: int32 [4096, 8], P(('req', 'kv')), may hold values from 0 to 127, all different within a row; in each aligned block of 32 rows (0 to 31, 32 to 63, ...) at most 4 rows name the same one
- gate_probs: float32 [4096, 8], P(('req', 'kv')), may hold values from 0.05 to 1
- w_gate: bfloat16 [128, 2048, 768], P(('req', 'kv')), may hold values from -0.125 to 0.125
- w_up: bfloat16 [128, 2048, 768], P(('req', 'kv')), may hold values from -0.125 to 0.125
- w_down: bfloat16 [128, 768, 2048], P(('req', 'kv')), may hold values from -0.21875 to 0.21875
Outputs:
- layer_out: bfloat16 [4096, 2048], P(('req', 'kv'))
- moved_keys: bfloat16 [64, 4, 1024, 128], P('req', 'kv')
- moved_values: bfloat16 [64, 4, 1024, 128], P('req', 'kv')
The draws below stay inside these ranges and needn't reach their ends.
Inputs may be any that keep to these rules, and one draw needn't show every extreme that they name: `lengths`: in each block of 128 requests of one index of req, between 2 and 16 requests are longer than 64 tokens and the others are at most 64 long; some request is exactly 1024 long. `page_table`: entries j below the ceiling of lengths[r] / 64 name distinct pages of the pool of request r's own index of req, counted within that pool; later entries are arbitrary pages of that pool. `mig_slot`: row g names 2 distinct local rows of index g of req, each a request longer than 64 tokens. `routes`: in the rows of one device (aligned blocks of 32 rows) no expert is named by more than 4 rows.
All inputs are finite; a program needn't handle non-finite values.
Results may differ from the reference program's by a relative error of at most 0.011.
Values may be sent and summed in bfloat16 or wider, within the bound.
No kernel may reach another device: no remote copies, remote signals or barrier semaphores. Data moves between devices by JAX's collectives and lax.ppermute only.
A program may use at most 128 MiB of HBM per device.

```python
import math
import jax
import jax.numpy as jnp
import numpy as np
from jax import lax

MODEL_DIMENSION = 2048
HQ = 32
KEY_VALUE_HEADS = 4
HEAD_DIMENSION = 128
FFN = 768
TOPK = 8
REQ_DEV = 128
PAGE_TOKENS = 64
MAXP = 16
MIG_DEV = 2
EXPERTS = 128
QUERY_PER_KEY = 8
REQUEST_COUNT = 4096
DISP_DEV = 32
MAX_TOKENS = 1024
POOL_DEV = 368
TOTAL_PAGES = 11776
MOVING_REQUESTS = 64
CAP = 4
ROWS_EXPERT = 512
N_REQ = 32


def request_plan(key):
    groups = REQUEST_COUNT // REQ_DEV
    random_subkeys = jax.random.split(jax.random.fold_in(key, 101), 6)
    long_most = REQ_DEV // 8
    heavy_dev = jax.random.randint(random_subkeys[0], (groups,), 0, 8) == 0
    forced = jax.random.randint(random_subkeys[1], (), 0, groups)
    heavy_dev = heavy_dev | (jnp.arange(groups) == forced)
    light_count = jnp.minimum(jax.random.randint(random_subkeys[2], (groups,), 0, 2), long_most - MIG_DEV)
    long_count = MIG_DEV + jnp.where(heavy_dev, long_most - MIG_DEV, light_count)
    scores = jax.random.randint(random_subkeys[3], (groups, REQ_DEV), 0, REQ_DEV) * REQ_DEV + jnp.arange(REQ_DEV)[None, :]
    ordering = jnp.argsort(scores, axis=1)
    ranking = jnp.argsort(ordering, axis=1)
    is_long = ranking < long_count[:, None]
    short_len = jax.random.randint(random_subkeys[4], (groups, REQ_DEV), 1, PAGE_TOKENS + 1)
    longer = jax.random.randint(random_subkeys[5], (groups, REQ_DEV), MAX_TOKENS // 2 + 1, MAX_TOKENS + 1)
    longer = jnp.where((ranking == 0) & (jnp.arange(groups) == forced)[:, None], MAX_TOKENS, longer)
    lengths = jnp.where(is_long, longer, short_len).astype(jnp.int32)
    return (lengths, ordering[:, :MIG_DEV].astype(jnp.int32))


def draw_lengths(key, part):
    lengths, departing = request_plan(key)
    return lengths.reshape(-1)


def draw_mig_slot(key, part):
    lengths, departing = request_plan(key)
    return departing


def draw_page_table(key, part):
    lengths, departing = request_plan(key)
    groups = lengths.shape[0]
    random_subkeys = jax.random.split(jax.random.fold_in(key, 202), 2)
    needed = (lengths + PAGE_TOKENS - 1) // PAGE_TOKENS
    offsets = jnp.cumsum(needed, axis=1) - needed
    shuffled = jnp.argsort(jax.random.randint(random_subkeys[0], (groups, POOL_DEV), 0, POOL_DEV) * POOL_DEV + jnp.arange(POOL_DEV)[None, :], axis=1)
    entry_index = offsets[:, :, None] + jnp.arange(MAXP)[None, None, :]
    chosen = jnp.take_along_axis(shuffled, jnp.minimum(entry_index, POOL_DEV - 1).reshape(groups, -1), axis=1).reshape(groups, REQ_DEV, MAXP)
    filler = jax.random.randint(random_subkeys[1], (groups, REQ_DEV, MAXP), 0, POOL_DEV)
    page_rows = jnp.where(jnp.arange(MAXP)[None, None, :] < needed[:, :, None], chosen, filler)
    return page_rows.reshape(REQUEST_COUNT, MAXP).astype(jnp.int32)


def draw_key_cache(key, part):
    random_subkeys = jax.random.split(jax.random.fold_in(key, 303), 1)
    gaussian_part = jnp.clip(jax.random.normal(random_subkeys[0], (TOTAL_PAGES, KEY_VALUE_HEADS, PAGE_TOKENS, HEAD_DIMENSION), jnp.float32), -4.0, 4.0)
    return gaussian_part.astype(jnp.bfloat16)


def shard_levels(stream_key, shape, cuts, smallest, top_value):
    def one(dim, parts):
        draws = jax.random.uniform(jax.random.fold_in(jax.random.fold_in(stream_key, 6), dim), (parts,), jnp.float32, smallest / len(cuts), top_value / len(cuts))
        return jnp.repeat(jnp.exp(draws), shape[dim] // parts).reshape((-1,) + (1,) * (len(shape) - dim - 1))

    gain = one(*cuts[0])
    for cut in cuts[1:]:
        gain = gain * one(*cut)
    return gain


def shared_out(key, own, number, rows, count, top, most, slope):
    order = jax.random.permutation(key, count)
    crowded, common = load_shares(count, rows * top, most, slope, True), load_shares(count, rows * top, most, slope, False)
    places = jnp.arange(count)

    def named(sizes, turn):
        used = int((sizes > 0).sum())
        fixed = max(1, used // 4)
        moved = fixed + (places - fixed + turn * (used - fixed)) % max(1, count - fixed)
        return jnp.zeros((count,), jnp.int32).at[order[jnp.where(places < fixed, places, moved)]].set(jnp.asarray(sizes, jnp.int32))

    sizes = jnp.where(number % 4 == 0, named(crowded, number // 4), named(common, number - number // 4 - 1))
    mixed = jax.random.permutation(jax.random.fold_in(own, 3), count)
    source_of, receiver = mixed[0:count // 2 * 2:2], mixed[1:count // 2 * 2:2]
    slack = jnp.minimum(sizes[source_of] - 1, most - sizes[receiver]) // 2
    slack = jnp.where((source_of == order[0]) | (receiver == order[0]) | (sizes[receiver] == 0), 0, jnp.maximum(slack, 0))
    moved = jax.random.randint(jax.random.fold_in(own, 4), (count // 2,), 0, 1 << 20) % (slack + 1)
    sizes = sizes.at[source_of].add(-moved).at[receiver].add(moved)
    labels = jnp.searchsorted(jnp.cumsum(sizes), jnp.arange(rows * top), side="right").astype(jnp.int32)
    listing = labels.reshape(top, rows).T
    listing = listing[jax.random.permutation(jax.random.fold_in(own, 1), rows)]
    turn = jax.random.randint(jax.random.fold_in(own, 2), (rows, 1), 0, top)
    return jnp.take_along_axis(listing, (jnp.arange(top)[None, :] + turn) % top, axis=1)


def load_shares(number_of, total, most, lean, full):
    portions = [(1 << 20) // math.isqrt(grade ** lean) + 1 for grade in range(1, number_of + 1)]
    largest = most if full else min(most, max(-(-total // number_of), total * portions[0] // sum(portions)))
    least = 1 if total - largest >= number_of - 1 else 0
    given, surplus = [largest] + [least] * (number_of - 1), total - largest - least * (number_of - 1)
    while surplus > 0:
        candidates = [i for i in range(1, number_of) if given[i] < largest] or [i for i in range(1, number_of) if given[i] < most]
        pool, remaining = sum([portions[i] for i in candidates]), surplus
        for i in candidates:
            extra = min(most - given[i], max(1, remaining * portions[i] // pool), surplus)
            given[i] = given[i] + extra
            surplus = surplus - extra
    return np.array(given)


def gaussian(key, shape, deviation, most, cuts=(), kind=jnp.bfloat16):
    entries = deviation * jax.random.normal(key, shape, jnp.float32)
    if cuts:
        entries = entries * shard_levels(key, shape, cuts, -0.22, 0.18)
    return jnp.clip(entries, -most, most).astype(kind)


def setup_inputs(seed: int = 0) -> dict:
    streams_of = jax.random.split(jax.random.key(seed), 18)
    tokens = gaussian(streams_of[0], (REQUEST_COUNT, MODEL_DIMENSION), 1.0, 6.0, ((0, 32),))
    lengths = draw_lengths(jax.random.fold_in(streams_of[17], 71), 0)
    page_table = draw_page_table(jax.random.fold_in(streams_of[17], 71), 0)
    key_cache = draw_key_cache(jax.random.fold_in(streams_of[17], 71), 0)
    value_page_cache = gaussian(streams_of[4], (TOTAL_PAGES, KEY_VALUE_HEADS, PAGE_TOKENS, HEAD_DIMENSION), 1.0, 6.0, ((0, 32), (1, 4)))
    mig_slot = draw_mig_slot(jax.random.fold_in(streams_of[17], 71), 0)
    attn_gain = jnp.clip(1.0 + 0.18 * jax.random.normal(streams_of[6], (MODEL_DIMENSION,), jnp.float32), 0.1, 1.9)
    w_query = gaussian(streams_of[7], (MODEL_DIMENSION, HQ * HEAD_DIMENSION), MODEL_DIMENSION ** -0.5, 0.125, ((1, 4),))
    key_weight = gaussian(streams_of[8], (MODEL_DIMENSION, KEY_VALUE_HEADS * HEAD_DIMENSION), MODEL_DIMENSION ** -0.5, 0.125, ((1, 4),))
    value_weight = gaussian(streams_of[9], (MODEL_DIMENSION, KEY_VALUE_HEADS * HEAD_DIMENSION), MODEL_DIMENSION ** -0.5, 0.125, ((1, 4),))
    w_out = gaussian(streams_of[10], (HQ * HEAD_DIMENSION, MODEL_DIMENSION), (HQ * HEAD_DIMENSION) ** -0.5, 0.09375, ((0, 4),))
    moe_gain = jnp.clip(1.0 + 0.18 * jax.random.normal(streams_of[11], (MODEL_DIMENSION,), jnp.float32), 0.1, 1.9)
    routes_keys = jax.random.split(jax.random.fold_in(streams_of[12], 1), REQUEST_COUNT // DISP_DEV)
    routes_turns = jax.random.permutation(jax.random.fold_in(streams_of[12], 3), REQUEST_COUNT // DISP_DEV)
    routes = jax.vmap(lambda own, number: shared_out(jax.random.fold_in(streams_of[12], 2), own, number, DISP_DEV, EXPERTS, TOPK, CAP, 2))(routes_keys, routes_turns).reshape((REQUEST_COUNT, TOPK))
    gate_probs = jnp.clip(jnp.exp(math.log(1.0) - 2.9957323 * jax.random.uniform(streams_of[13], (REQUEST_COUNT, TOPK), jnp.float32) ** shard_levels(streams_of[13], (REQUEST_COUNT, TOPK), ((0, 128),), -0.2, 0.2)), 0.05, 1.0)
    w_gate = gaussian(streams_of[14], (EXPERTS, MODEL_DIMENSION, FFN), MODEL_DIMENSION ** -0.5, 0.125, ((0, 128),))
    w_up = gaussian(streams_of[15], (EXPERTS, MODEL_DIMENSION, FFN), MODEL_DIMENSION ** -0.5, 0.125, ((0, 128),))
    w_down = gaussian(streams_of[16], (EXPERTS, FFN, MODEL_DIMENSION), FFN ** -0.5, 0.21875, ((0, 128),))
    return dict(tokens=tokens, lengths=lengths, page_table=page_table, key_cache=key_cache, value_page_cache=value_page_cache, mig_slot=mig_slot, attn_gain=attn_gain, w_query=w_query, key_weight=key_weight, value_weight=value_weight, w_out=w_out, moe_gain=moe_gain, routes=routes, gate_probs=gate_probs, w_gate=w_gate, w_up=w_up, w_down=w_down)


EPSILON = 1e-06
THETA = 1000000.0

def rms_scale(inputs, gain_vec):
    return inputs * lax.rsqrt(lax.optimization_barrier(jnp.mean(inputs * inputs, axis=-1, keepdims=True)) + EPSILON) * gain_vec

def rotate(vectors, positions):
    half_width = vectors.shape[-1] // 2
    exponent = jnp.arange(half_width, dtype=jnp.float32) * (-2.0 / vectors.shape[-1])
    angles = positions.astype(jnp.float32)[..., None] * THETA ** exponent
    cosine = jnp.cos(angles)
    sine_part = jnp.sin(angles)
    front_half = vectors[..., :half_width]
    back_half = vectors[..., half_width:]
    return jnp.concatenate([front_half * cosine - back_half * sine_part, back_half * cosine + front_half * sine_part], axis=-1)

def reference(tokens, lengths, page_table, key_cache, value_page_cache, mig_slot, attn_gain, w_query, key_weight, value_weight, w_out, moe_gain, routes, gate_probs, w_gate, w_up, w_down):
    normalized_rows = rms_scale(tokens.astype(jnp.float32), attn_gain).astype(jnp.bfloat16)
    queries = jnp.dot(normalized_rows, w_query, preferred_element_type=jnp.float32).reshape(REQUEST_COUNT, HQ, HEAD_DIMENSION)
    fresh_key = jnp.dot(normalized_rows, key_weight, preferred_element_type=jnp.float32).reshape(REQUEST_COUNT, KEY_VALUE_HEADS, HEAD_DIMENSION)
    fresh_value = jnp.dot(normalized_rows, value_weight, preferred_element_type=jnp.float32).reshape(REQUEST_COUNT, KEY_VALUE_HEADS, HEAD_DIMENSION).astype(jnp.bfloat16)
    queries = rotate(rms_scale(queries, 1.0), lengths[:, None]).astype(jnp.bfloat16)
    fresh_key = rotate(rms_scale(fresh_key, 1.0), lengths[:, None]).astype(jnp.bfloat16)
    devices_of = (jnp.arange(REQUEST_COUNT, dtype=jnp.int32) // REQ_DEV).astype(jnp.int32)
    scale_factor = 1.0 / math.sqrt(HEAD_DIMENSION)

    def one_request(packed):
        query_matrix, key_row, value_row, page_rows, length, device = packed
        rows_index = (device * POOL_DEV + page_rows).astype(jnp.int32)
        stored_keys = jnp.take(key_cache, rows_index, axis=0)
        stored_keys = jnp.transpose(stored_keys, (1, 0, 2, 3)).reshape(KEY_VALUE_HEADS, MAX_TOKENS, HEAD_DIMENSION).astype(jnp.float32)
        stored_values = jnp.take(value_page_cache, rows_index, axis=0)
        stored_values = jnp.transpose(stored_values, (1, 0, 2, 3)).reshape(KEY_VALUE_HEADS, MAX_TOKENS, HEAD_DIMENSION).astype(jnp.float32)
        query_groups = query_matrix.reshape(KEY_VALUE_HEADS, QUERY_PER_KEY, HEAD_DIMENSION).astype(jnp.float32)
        scores = jnp.einsum('kgh,kth->kgt', query_groups, stored_keys) * scale_factor
        self_score = jnp.einsum('kgh,kh->kg', query_groups, key_row.astype(jnp.float32)) * scale_factor
        usable = jnp.arange(MAX_TOKENS) < length
        best_score = jnp.maximum(self_score, lax.optimization_barrier(jnp.max(jnp.where(usable, scores, -jnp.inf), axis=2)))
        weights = jnp.where(usable, jnp.exp(jnp.minimum(scores - best_score[:, :, None], 0.0)), 0.0)
        self_weight = jnp.exp(self_score - best_score)
        denominator = lax.optimization_barrier(jnp.sum(weights, axis=2)) + self_weight
        rounded = lax.optimization_barrier(weights.astype(jnp.bfloat16)).astype(jnp.float32)
        rounded_self = lax.optimization_barrier(self_weight.astype(jnp.bfloat16)).astype(jnp.float32)
        summed = jnp.einsum('kgt,kth->kgh', rounded, stored_values)
        summed = summed + rounded_self[:, :, None] * value_row.astype(jnp.float32)[:, None, :]
        return (summed / denominator[:, :, None]).reshape(HQ * HEAD_DIMENSION).astype(jnp.bfloat16)
    attended = lax.map(one_request, (queries, fresh_key, fresh_value, page_table, lengths, devices_of))
    hidden = (tokens.astype(jnp.float32) + jnp.dot(attended, w_out, preferred_element_type=jnp.float32)).astype(jnp.bfloat16)
    group_index = jnp.arange(N_REQ, dtype=jnp.int32)
    partner = ((group_index + N_REQ // 2) % N_REQ).astype(jnp.int32)
    target_rows = (group_index[:, None] * REQ_DEV + mig_slot).reshape(-1).astype(jnp.int32)
    source_rows = (partner[:, None] * REQ_DEV + jnp.take(mig_slot, partner, axis=0)).reshape(-1).astype(jnp.int32)
    placed = jnp.arange(REQUEST_COUNT, dtype=jnp.int32).at[target_rows].set(source_rows)
    settled = jnp.take(hidden, placed, axis=0)
    moved_rows = ((source_rows // REQ_DEV)[:, None] * POOL_DEV + jnp.take(page_table, source_rows, axis=0)).astype(jnp.int32)
    moved_mask = jnp.arange(MAX_TOKENS)[None, :] < jnp.take(lengths, source_rows)[:, None]

    def gather_moved(cache_pool):
        collected_rows = jnp.take(cache_pool, moved_rows, axis=0)
        collected_rows = jnp.transpose(collected_rows, (0, 2, 1, 3, 4)).reshape(MOVING_REQUESTS, KEY_VALUE_HEADS, MAX_TOKENS, HEAD_DIMENSION)
        return jnp.where(moved_mask[:, None, :, None], collected_rows, jnp.zeros((), jnp.bfloat16))
    moe_in = rms_scale(settled.astype(jnp.float32), moe_gain).astype(jnp.bfloat16)
    flat_routes = routes.reshape(-1).astype(jnp.int32)
    ordering = jnp.argsort(flat_routes, stable=True).astype(jnp.int32)
    counts = lax.optimization_barrier(jnp.sum((flat_routes[:, None] == jnp.arange(EXPERTS, dtype=jnp.int32)[None, :]).astype(jnp.int32), axis=0))
    starts = (jnp.cumsum(counts) - counts).astype(jnp.int32)
    padded_order = jnp.concatenate([ordering, jnp.zeros((ROWS_EXPERT,), jnp.int32)])

    def one_expert(packed):
        expert, first_row, amount = packed
        picked = lax.dynamic_slice_in_dim(padded_order, first_row, ROWS_EXPERT)
        rows_in = jnp.take(moe_in, picked // TOPK, axis=0)
        gate_part = jnp.dot(rows_in, w_gate[expert], preferred_element_type=jnp.float32)
        up_part = jnp.dot(rows_in, w_up[expert], preferred_element_type=jnp.float32)
        activated = (jax.nn.silu(gate_part) * up_part).astype(jnp.bfloat16)
        produced = jnp.dot(activated, w_down[expert], preferred_element_type=jnp.float32).astype(jnp.bfloat16)
        filled = jnp.arange(ROWS_EXPERT) < amount
        return (produced, jnp.where(filled, picked, REQUEST_COUNT * TOPK).astype(jnp.int32))
    produced, targets = lax.map(one_expert, (jnp.arange(EXPERTS, dtype=jnp.int32), starts, counts))
    expert_out = jnp.zeros((REQUEST_COUNT * TOPK + 1, MODEL_DIMENSION), jnp.bfloat16).at[targets.reshape(-1)].set(produced.reshape(-1, MODEL_DIMENSION))
    expert_out = expert_out[:REQUEST_COUNT * TOPK].reshape(REQUEST_COUNT, TOPK, MODEL_DIMENSION)
    shares = gate_probs / lax.optimization_barrier(jnp.sum(gate_probs, axis=1, keepdims=True))
    mixed_rows = settled.astype(jnp.float32) + lax.optimization_barrier(jnp.sum(shares[:, :, None] * expert_out.astype(jnp.float32), axis=1))
    return (mixed_rows.astype(jnp.bfloat16), gather_moved(key_cache), gather_moved(value_page_cache))
```

```python
import math

import jax
import jax.numpy as jnp
from jax import lax
from jax.experimental import pallas as pl
from jax.experimental.pallas import tpu as pltpu
from jax.sharding import PartitionSpec as P

EPSILON = 1e-06
THETA = 1000000.0
MASKED = -1e30
BF16 = jnp.bfloat16
F32 = jnp.float32
POOL_CUTS = 4
QUERY_CUTS = 4
GROUP = 4
UNROLL_SHORT = 4
UNROLL_LONG = 2


def dot_t(a, b):
    return lax.dot_general(a, b, (((1,), (1,)), ((), ())), preferred_element_type=F32)


def dot_n(a, b):
    return jnp.dot(a, b, preferred_element_type=F32)


def attention_kernel(
    table,
    lens,
    slots,
    tokens,
    gain,
    cos_ref,
    sin_ref,
    wq_hbm,
    wk_hbm,
    wv_hbm,
    k_hbm,
    v_hbm,
    att_out,
    mig_out,
    dk_out,
    dv_out,
    wq,
    wk,
    wv,
    kp,
    vp,
    qs,
    ks,
    vs,
    os,
    mig,
    longs,
    wsem,
    psem,
):
    rows, width = tokens.shape
    pool, page, head = kp.shape
    max_pages = table.shape[1]
    heads = wq.shape[1] // head
    scale = 1.0 / math.sqrt(head)
    wcut = wq.shape[1] // QUERY_CUTS
    pcut = pool // POOL_CUTS

    wcopies = [
        pltpu.make_async_copy(
            wq_hbm.at[:, pl.ds(c * wcut, wcut)], wq.at[:, pl.ds(c * wcut, wcut)], wsem.at[c]
        )
        for c in range(QUERY_CUTS)
    ]
    wcopies.append(pltpu.make_async_copy(wk_hbm, wk, wsem.at[QUERY_CUTS]))
    wcopies.append(pltpu.make_async_copy(wv_hbm, wv, wsem.at[QUERY_CUTS + 1]))
    pcopies = []
    for i, (src, dst) in enumerate(((k_hbm, kp), (v_hbm, vp))):
        for c in range(POOL_CUTS):
            pcopies.append(
                pltpu.make_async_copy(
                    src.at[pl.ds(c * pcut, pcut), 0],
                    dst.at[pl.ds(c * pcut, pcut)],
                    psem.at[i * POOL_CUTS + c],
                )
            )
    for copy in wcopies + pcopies:
        copy.start()

    def gather_long(r, n):
        is_long = lens[r] > page

        @pl.when(is_long)
        def _():
            longs[n] = r

        return n + is_long.astype(jnp.int32)

    long_count = lax.fori_loop(0, rows, gather_long, jnp.int32(0))

    x = tokens[...].astype(F32)
    row_id = lax.broadcasted_iota(jnp.int32, (rows, 1), 0)
    for k in range(2):
        leaving = jnp.sum(jnp.where(row_id == slots[k], x, 0.0), axis=0, keepdims=True)
        for c in range(width // head):
            mig[k * 24 + 8 + c : k * 24 + 9 + c, :] = leaving[:, c * head : (c + 1) * head]
    normed = (
        x * lax.rsqrt(jnp.mean(x * x, axis=-1, keepdims=True) + EPSILON) * gain[...]
    ).astype(BF16)
    cos = cos_ref[...]
    sin = sin_ref[...]

    def rotated(vectors):
        unit = vectors * lax.rsqrt(jnp.mean(vectors * vectors, axis=-1, keepdims=True) + EPSILON)
        turned = unit * cos + pltpu.roll(unit, head // 2, 1) * sin
        return turned.astype(BF16).astype(F32)

    per_cut = wcut // head
    for c in range(QUERY_CUTS):
        wcopies[c].wait()
        query = dot_n(normed, wq[:, c * wcut : (c + 1) * wcut])
        for i in range(per_cut):
            qs[pl.ds(c * per_cut + i, rows, stride=heads), :] = rotated(
                query[:, i * head : (i + 1) * head]
            )
    wcopies[QUERY_CUTS].wait()
    wcopies[QUERY_CUTS + 1].wait()
    fresh_key = rotated(dot_n(normed, wk[...]))
    fresh_value = dot_n(normed, wv[...]).astype(BF16).astype(F32)
    for h in range(heads):
        ks[pl.ds(h, rows, stride=heads), :] = fresh_key
        vs[pl.ds(h, rows, stride=heads), :] = fresh_value

    for copy in pcopies:
        copy.wait()

    def softmax_out(query, base, count, scores, valid, values):
        scores = jnp.where(valid, scores * scale, MASKED)
        self_score = jnp.sum(query * ks[pl.ds(base, count), :], axis=1, keepdims=True) * scale
        top = jnp.maximum(jnp.max(scores, axis=1, keepdims=True), self_score)
        weights = jnp.exp(scores - top)
        self_weight = jnp.exp(self_score - top)
        total = jnp.sum(weights, axis=1, keepdims=True) + self_weight
        summed = dot_n(weights.astype(BF16), values)
        summed = summed + self_weight.astype(BF16).astype(F32) * vs[pl.ds(base, count), :]
        os[pl.ds(base, count), :] = summed / total

    lanes = lax.broadcasted_iota(jnp.int32, (GROUP * heads, GROUP * page), 1)
    subs = lax.broadcasted_iota(jnp.int32, (GROUP * heads, GROUP * page), 0)
    place = jnp.where(lanes // page == subs // heads, lanes % page, 1 << 20)
    lane_row = lax.broadcasted_iota(jnp.int32, (1, GROUP * page), 1)

    def short_group(g):
        first = g * GROUP
        base = pl.multiple_of(first * heads, GROUP * heads)
        pages = [table[first + i, 0] for i in range(GROUP)]
        keys = jnp.concatenate([kp[p] for p in pages], axis=0)
        values = jnp.concatenate([vp[p] for p in pages], axis=0)
        limit = jnp.full((1, GROUP * page), lens[first], jnp.int32)
        for i in range(1, GROUP):
            limit = jnp.where(lane_row >= i * page, lens[first + i], limit)
        query = qs[pl.ds(base, GROUP * heads), :]
        scores = dot_t(query.astype(BF16), keys)
        softmax_out(query, base, GROUP * heads, scores, place < limit, values)

    def short_step(step, carry):
        for u in range(UNROLL_SHORT):
            short_group(step * UNROLL_SHORT + u)
        return carry

    lax.fori_loop(0, rows // (GROUP * UNROLL_SHORT), short_step, 0)

    span = lax.broadcasted_iota(jnp.int32, (heads, max_pages * page), 1)

    def long_one(r):
        base = pl.multiple_of(r * heads, heads)
        query = qs[pl.ds(base, heads), :]
        query16 = query.astype(BF16)
        pages = [table[r, j] for j in range(max_pages)]
        scores = []
        for c in range(max_pages // 4):
            keys = jnp.concatenate([kp[pages[c * 4 + i]] for i in range(4)], axis=0)
            scores.append(dot_t(query16, keys))
        scores = jnp.concatenate(scores, axis=1)
        values = jnp.concatenate([vp[p] for p in pages], axis=0)
        softmax_out(query, base, heads, scores, span < lens[r], values)

    def long_step(step, carry):
        for u in range(UNROLL_LONG):
            long_one(longs[jnp.minimum(step * UNROLL_LONG + u, long_count - 1)])
        return carry

    lax.fori_loop(0, (long_count + UNROLL_LONG - 1) // UNROLL_LONG, long_step, 0)

    for h in range(heads):
        att_out[:, h * head : (h + 1) * head] = os[pl.ds(h, rows, stride=heads), :].astype(BF16)
    for k in range(2):
        mig[k * 24 : k * 24 + 8, :] = os[pl.ds(pl.multiple_of(slots[k] * heads, heads), heads), :]
    mig_out[...] = mig[...].astype(BF16)

    in_page = lax.broadcasted_iota(jnp.int32, (page, head), 0)
    for k in range(2):

        def depart(j, carry, k=k):
            row = slots[k]
            held = table[row, j]
            keep = in_page < lens[row] - j * page
            at = pl.multiple_of(j * page, page)
            dk_out[k, pl.ds(at, page), :] = jnp.where(keep, kp[held].astype(F32), 0.0).astype(BF16)
            dv_out[k, pl.ds(at, page), :] = jnp.where(keep, vp[held].astype(F32), 0.0).astype(BF16)
            return carry

        lax.fori_loop(0, max_pages, depart, 0)


def attention(table, lens, slots, tokens, gain, cos, sin, wq, wk, wv, kc, vc):
    rows, width = tokens.shape
    pool, _, page, head = kc.shape
    heads = wq.shape[1] // head
    span = table.shape[1] * page
    smem = pl.BlockSpec(memory_space=pltpu.SMEM)
    vmem = pl.BlockSpec(memory_space=pltpu.VMEM)
    anyspace = pl.BlockSpec(memory_space=pl.ANY)
    return pl.pallas_call(
        attention_kernel,
        out_shape=(
            jax.ShapeDtypeStruct((rows, heads * head), BF16),
            jax.ShapeDtypeStruct((48, head), BF16),
            jax.ShapeDtypeStruct((2, span, head), BF16),
            jax.ShapeDtypeStruct((2, span, head), BF16),
        ),
        in_specs=[smem, smem, smem, vmem, vmem, vmem, vmem] + [anyspace] * 5,
        out_specs=(vmem, vmem, vmem, vmem),
        scratch_shapes=[
            pltpu.VMEM(wq.shape, BF16),
            pltpu.VMEM(wk.shape, BF16),
            pltpu.VMEM(wv.shape, BF16),
            pltpu.VMEM((pool, page, head), BF16),
            pltpu.VMEM((pool, page, head), BF16),
            pltpu.VMEM((rows * heads, head), F32),
            pltpu.VMEM((rows * heads, head), F32),
            pltpu.VMEM((rows * heads, head), F32),
            pltpu.VMEM((rows * heads, head), F32),
            pltpu.VMEM((48, head), F32),
            pltpu.SMEM((rows,), jnp.int32),
            pltpu.SemaphoreType.DMA((QUERY_CUTS + 2,)),
            pltpu.SemaphoreType.DMA((2 * POOL_CUTS,)),
        ],
        compiler_params=pltpu.CompilerParams(vmem_limit_bytes=40 << 20),
        name="attention",
    )(table, lens, slots, tokens, gain, cos, sin, wq, wk, wv, kc, vc)


def project_kernel(slots, attended, arrived, w_out, partial):
    rows, _ = attended.shape
    head = arrived.shape[1]
    heads = attended.shape[1] // head
    row_id = lax.broadcasted_iota(jnp.int32, (rows, head), 0)
    got = arrived[...].astype(F32)
    pieces = []
    for h in range(heads):
        piece = attended[:, h * head : (h + 1) * head].astype(F32)
        for k in range(2):
            piece = jnp.where(row_id == slots[k], got[k * 24 + h : k * 24 + h + 1, :], piece)
        pieces.append(piece.astype(BF16))
    settled = jnp.concatenate(pieces, axis=1)
    partial[...] = dot_n(settled, w_out[...]).astype(BF16)


def project(slots, attended, arrived, w_out):
    vmem = pl.BlockSpec(memory_space=pltpu.VMEM)
    return pl.pallas_call(
        project_kernel,
        out_shape=jax.ShapeDtypeStruct((attended.shape[0], w_out.shape[1]), BF16),
        in_specs=[pl.BlockSpec(memory_space=pltpu.SMEM), vmem, vmem, vmem],
        out_specs=vmem,
        compiler_params=pltpu.CompilerParams(vmem_limit_bytes=24 << 20),
        name="project",
    )(slots, attended, arrived, w_out)


def expert_kernel(received, wg, wu, wd, out, xs):
    pairs = received.shape[0] // 16
    half = received.shape[1]
    cut = 256
    low = lax.broadcasted_iota(jnp.int32, (pairs, 8, cut), 1) < 4
    for c in range(half // cut):
        part = received[:, c * cut : (c + 1) * cut].astype(F32).reshape(pairs, 2, 8, cut)
        one, two = part[:, 0], part[:, 1]
        left = jnp.where(low, one, pltpu.roll(two, 4, 1))
        right = jnp.where(low, pltpu.roll(one, 4, 1), two)
        xs[:, c * cut : (c + 1) * cut] = left.reshape(pairs * 8, cut).astype(BF16)
        xs[:, half + c * cut : half + (c + 1) * cut] = right.reshape(pairs * 8, cut).astype(BF16)
    inputs = xs[...]
    gate = dot_n(inputs, wg[0])
    up = dot_n(inputs, wu[0])
    act = (gate / (1.0 + jnp.exp(-gate)) * up).astype(BF16)
    for c in range(half // cut):
        left = dot_n(act, wd[0, :, c * cut : (c + 1) * cut]).reshape(pairs, 8, cut)
        right = dot_n(act, wd[0, :, half + c * cut : half + (c + 1) * cut]).reshape(pairs, 8, cut)
        one = jnp.where(low, left, pltpu.roll(right, 4, 1))
        two = jnp.where(low, pltpu.roll(left, 4, 1), right)
        both = jnp.stack([one, two], axis=1).reshape(pairs * 16, cut)
        out[:, c * cut : (c + 1) * cut] = both.astype(BF16)


def expert(received, wg, wu, wd):
    vmem = pl.BlockSpec(memory_space=pltpu.VMEM)
    rows, half = received.shape
    return pl.pallas_call(
        expert_kernel,
        out_shape=jax.ShapeDtypeStruct((rows, half), BF16),
        in_specs=[vmem] * 4,
        out_specs=vmem,
        scratch_shapes=[pltpu.VMEM((rows // 2, 2 * half), BF16)],
        compiler_params=pltpu.CompilerParams(vmem_limit_bytes=40 << 20),
        name="expert",
    )(received, wg, wu, wd)


def body(
    tokens,
    lengths,
    page_table,
    key_cache,
    value_page_cache,
    mig_slot,
    attn_gain,
    w_query,
    key_weight,
    value_weight,
    w_out,
    moe_gain,
    routes,
    gate_probs,
    w_gate,
    w_up,
    w_down,
):
    req_count = lax.axis_size("req")
    kv_count = lax.axis_size("kv")
    req_here = lax.axis_index("req")
    kv_here = lax.axis_index("kv")
    requests_here, model_width = tokens.shape
    head = key_weight.shape[1]
    half = model_width // 2
    lens = lax.dynamic_slice_in_dim(lengths, req_here * requests_here, requests_here)
    slots = lax.dynamic_index_in_dim(mig_slot, req_here, 0, keepdims=False)
    exponent = jnp.arange(head // 2, dtype=F32) * (-2.0 / head)
    angles = lens.astype(F32)[:, None] * THETA**exponent
    cosine, sine = jnp.cos(angles), jnp.sin(angles)
    attended, leaving, depart_keys, depart_values = attention(
        page_table,
        lens,
        slots,
        tokens,
        attn_gain[None, :],
        jnp.concatenate([cosine, cosine], axis=1),
        jnp.concatenate([-sine, sine], axis=1),
        w_query,
        key_weight,
        value_weight,
        key_cache,
        value_page_cache,
    )
    swap = [(i, (i + req_count // 2) % req_count) for i in range(req_count)]
    arrived = lax.ppermute(leaving, "req", swap)
    arrived_keys = lax.ppermute(depart_keys, "req", swap)
    arrived_values = lax.ppermute(depart_values, "req", swap)
    partial = project(slots, attended, arrived, w_out)

    disp_rows = requests_here // kv_count
    partial = partial.reshape(kv_count, disp_rows, model_width)
    total = lax.dynamic_index_in_dim(partial, kv_here, 0, keepdims=False).astype(F32)
    for s in range(1, kv_count):
        block = lax.dynamic_index_in_dim(partial, (kv_here + s) % kv_count, 0, keepdims=False)
        ring = [(i, (i + s) % kv_count) for i in range(kv_count)]
        total = total + lax.ppermute(block, "kv", ring).astype(F32)
    own = lax.dynamic_slice_in_dim(tokens, kv_here * disp_rows, disp_rows)
    row_ids = kv_here * disp_rows + jnp.arange(disp_rows, dtype=jnp.int32)
    arrived_rows = arrived.reshape(2, 24, head)[:, 8:].reshape(2, model_width)
    for k in range(2):
        own = jnp.where((row_ids == slots[k])[:, None], arrived_rows[k][None, :], own)
    hidden = (own.astype(F32) + total).astype(BF16)
    hidden32 = hidden.astype(F32)
    moe_in = (
        hidden32 * lax.rsqrt(jnp.mean(hidden32 * hidden32, axis=-1, keepdims=True) + EPSILON) * moe_gain
    ).astype(BF16)

    devices = req_count * kv_count
    top_count = routes.shape[1]
    capacity = 2 * disp_rows * top_count // devices
    flat_routes = routes.reshape(-1)
    ids = jnp.arange(disp_rows * top_count, dtype=jnp.int32)
    earlier = (flat_routes[:, None] == flat_routes[None, :]) & (ids[None, :] < ids[:, None])
    ranking = jnp.sum(earlier.astype(jnp.int32), axis=1)
    slot_index = (flat_routes * capacity + ranking).reshape(disp_rows, top_count)
    chunk_rows = 2 * capacity
    places = jnp.arange(devices * chunk_rows, dtype=jnp.int32)
    place_slot = (places // chunk_rows) * capacity + places % capacity
    place_half = (places % chunk_rows) // capacity
    hits = place_slot[None, None, :] == slot_index[:, :, None]
    shares = gate_probs / jnp.sum(gate_probs, axis=1, keepdims=True)
    share_map = jnp.sum(jnp.where(hits, shares[:, :, None], 0.0), axis=1)
    hit_map = jnp.any(hits, axis=1)
    halves = place_half[None, :] == jnp.arange(2, dtype=jnp.int32)[:, None]
    both_hits = (halves[:, None, :] & hit_map[None, :, :]).reshape(2 * disp_rows, -1).astype(BF16)
    both_shares = jnp.where(halves[:, None, :], share_map[None, :, :], 0.0).reshape(2 * disp_rows, -1)
    share_high = both_shares.astype(BF16)
    share_low = (both_shares - share_high.astype(F32)).astype(BF16)
    share_rows = jnp.concatenate([share_high, share_low], axis=0)

    stacked = jnp.concatenate([moe_in[:, :half], moe_in[:, half:]], axis=0)
    outgoing = lax.dot_general(
        both_hits, stacked, (((0,), (0,)), ((), ())), preferred_element_type=F32
    ).astype(BF16)
    outgoing = outgoing.reshape(devices, chunk_rows, half)
    received = lax.all_to_all(outgoing, ("req", "kv"), split_axis=0, concat_axis=0, tiled=True)
    made = expert(received.reshape(devices * chunk_rows, half), w_gate, w_up, w_down)
    returned = lax.all_to_all(
        made.reshape(devices, chunk_rows, half), ("req", "kv"), split_axis=0, concat_axis=0, tiled=True
    )
    mixed = dot_n(share_rows, returned.reshape(devices * chunk_rows, half))
    mixed = mixed[: 2 * disp_rows] + mixed[2 * disp_rows :]
    mixed = jnp.concatenate([mixed[:disp_rows], mixed[disp_rows:]], axis=1)
    layer_out = (hidden32 + mixed).astype(BF16)
    return (layer_out, arrived_keys[:, None], arrived_values[:, None])


def solution(mesh):
    in_specs = (
        P("req", None),
        P(),
        P("req", None),
        P("req", "kv", None, None),
        P("req", "kv", None, None),
        P(),
        P(),
        P(None, "kv"),
        P(None, "kv"),
        P(None, "kv"),
        P("kv", None),
        P(),
        P(("req", "kv"), None),
        P(("req", "kv"), None),
        P(("req", "kv"), None, None),
        P(("req", "kv"), None, None),
        P(("req", "kv"), None, None),
    )
    out_specs = (P(("req", "kv"), None), P("req", "kv", None, None), P("req", "kv", None, None))
    return jax.shard_map(body, mesh=mesh, in_specs=in_specs, out_specs=out_specs, check_vma=False)
```

```python
import math

import jax
import jax.numpy as jnp
from jax import lax
from jax.experimental import pallas as pl
from jax.experimental.pallas import tpu as pltpu
from jax.sharding import PartitionSpec as P

EPSILON = 1e-06
THETA = 1000000.0
MASKED = -1e30
BF16 = jnp.bfloat16
F32 = jnp.float32
POOL_CUTS = 4
QUERY_CUTS = 4
OUT_CUTS = 4
GROUP = 4
UNROLL_SHORT = 8
UNROLL_LONG = 4


def dot_t(a, b):
    return lax.dot_general(a, b, (((1,), (1,)), ((), ())), preferred_element_type=F32)


def dot_n(a, b):
    return jnp.dot(a, b, preferred_element_type=F32)


def in_hbm(x):
    return pltpu.with_memory_space_constraint(x, pltpu.HBM)


def attention_kernel(
    table_hbm,
    lens_hbm,
    slots_hbm,
    tokens_hbm,
    gain_hbm,
    wq_hbm,
    wk_hbm,
    wv_hbm,
    k_hbm,
    v_hbm,
    att_out,
    mig_out,
    dk_out,
    dv_out,
    table,
    lens,
    lens_row,
    slots,
    tokens,
    gain,
    wq,
    wk,
    wv,
    kp,
    vp,
    qs,
    ks,
    vs,
    os,
    mig,
    longs,
    isem,
    wsem,
    psem,
):
    rows, width = tokens.shape
    pool, page, head = kp.shape
    max_pages = table.shape[0]
    heads = wq.shape[1] // head
    scale = 1.0 / math.sqrt(head)
    wcut = wq.shape[1] // QUERY_CUTS
    pcut = pool // POOL_CUTS
    req = lax.axis_index("req")

    icopies = [
        pltpu.make_async_copy(tokens_hbm, tokens, isem.at[0]),
        pltpu.make_async_copy(gain_hbm, gain, isem.at[1]),
        pltpu.make_async_copy(lens_hbm.at[pl.ds(req, 1)], lens_row, isem.at[2]),
        pltpu.make_async_copy(lens_hbm.at[pl.ds(req, 1)], lens, isem.at[3]),
        pltpu.make_async_copy(table_hbm, table, isem.at[4]),
        pltpu.make_async_copy(slots_hbm, slots, isem.at[5]),
    ]
    wcopies = [
        pltpu.make_async_copy(
            wq_hbm.at[:, pl.ds(c * wcut, wcut)], wq.at[:, pl.ds(c * wcut, wcut)], wsem.at[c]
        )
        for c in range(QUERY_CUTS)
    ]
    wcopies.append(pltpu.make_async_copy(wk_hbm, wk, wsem.at[QUERY_CUTS]))
    wcopies.append(pltpu.make_async_copy(wv_hbm, wv, wsem.at[QUERY_CUTS + 1]))
    pcopies = []
    for i, (src, dst) in enumerate(((k_hbm, kp), (v_hbm, vp))):
        for c in range(POOL_CUTS):
            pcopies.append(
                pltpu.make_async_copy(
                    src.at[pl.ds(c * pcut, pcut), 0],
                    dst.at[pl.ds(c * pcut, pcut)],
                    psem.at[i * POOL_CUTS + c],
                )
            )
    for copy in icopies + wcopies + pcopies:
        copy.start()
    for copy in icopies:
        copy.wait()

    def gather_long(r, n):
        is_long = lens[0, r] > page

        @pl.when(is_long)
        def _():
            longs[n] = r

        return n + is_long.astype(jnp.int32)

    long_count = lax.fori_loop(0, rows, gather_long, jnp.int32(0))

    positions = jnp.broadcast_to(lens_row[...], (rows, rows)).astype(F32).T
    half_lane = lax.broadcasted_iota(jnp.int32, (1, head), 1)
    exponent = (half_lane % (head // 2)).astype(F32) * (-2.0 / head)
    angles = positions * jnp.exp(exponent * math.log(THETA))
    cos = jnp.cos(angles)
    sin = jnp.where(half_lane < head // 2, -1.0, 1.0) * jnp.sin(angles)

    x = tokens[...].astype(F32)
    row_id = lax.broadcasted_iota(jnp.int32, (rows, 1), 0)
    for k in range(2):
        leaving = jnp.sum(jnp.where(row_id == slots[k, req], x, 0.0), axis=0, keepdims=True)
        for c in range(width // head):
            mig[k * 24 + 8 + c : k * 24 + 9 + c, :] = leaving[:, c * head : (c + 1) * head]
    normed = (
        x * lax.rsqrt(jnp.mean(x * x, axis=-1, keepdims=True) + EPSILON) * gain[...]
    ).astype(BF16)

    def rotated(vectors):
        unit = vectors * lax.rsqrt(jnp.mean(vectors * vectors, axis=-1, keepdims=True) + EPSILON)
        turned = unit * cos + pltpu.roll(unit, head // 2, 1) * sin
        return turned.astype(BF16).astype(F32)

    per_cut = wcut // head
    for c in range(QUERY_CUTS):
        wcopies[c].wait()
        query = dot_n(normed, wq[:, c * wcut : (c + 1) * wcut])
        for i in range(per_cut):
            qs[pl.ds(c * per_cut + i, rows, stride=heads), :] = rotated(
                query[:, i * head : (i + 1) * head]
            )
    wcopies[QUERY_CUTS].wait()
    wcopies[QUERY_CUTS + 1].wait()
    fresh_key = rotated(dot_n(normed, wk[...]))
    fresh_value = dot_n(normed, wv[...]).astype(BF16).astype(F32)
    for h in range(heads):
        ks[pl.ds(h, rows, stride=heads), :] = fresh_key
        vs[pl.ds(h, rows, stride=heads), :] = fresh_value

    for copy in pcopies:
        copy.wait()

    def finish(bases, queries, scores, valids, values):
        count = queries[0].shape[0]
        scores = [jnp.where(v, x * scale, MASKED) for v, x in zip(valids, scores)]
        selves = [
            jnp.sum(q * ks[pl.ds(b, count), :], axis=1, keepdims=True) * scale
            for b, q in zip(bases, queries)
        ]
        tops = [
            jnp.maximum(jnp.max(x, axis=1, keepdims=True), y) for x, y in zip(scores, selves)
        ]
        weights = [jnp.exp(x - t) for x, t in zip(scores, tops)]
        summed = [dot_n(w.astype(BF16), v()) for w, v in zip(weights, values)]
        selves = [jnp.exp(y - t) for y, t in zip(selves, tops)]
        totals = [jnp.sum(w, axis=1, keepdims=True) + y for w, y in zip(weights, selves)]
        for b, y, t, o in zip(bases, selves, totals, summed):
            fresh = y.astype(BF16).astype(F32) * vs[pl.ds(b, count), :]
            os[pl.ds(b, count), :] = (o + fresh) / t

    lanes = lax.broadcasted_iota(jnp.int32, (GROUP * heads, GROUP * page), 1)
    subs = lax.broadcasted_iota(jnp.int32, (GROUP * heads, GROUP * page), 0)
    place = jnp.where(lanes // page == subs // heads, lanes % page, 1 << 20)
    lane_row = lax.broadcasted_iota(jnp.int32, (1, GROUP * page), 1)

    def joined(pool_ref, pages):
        return jnp.concatenate([pool_ref[p] for p in pages], axis=0)

    def short_step(step, carry):
        firsts = [(step * UNROLL_SHORT + u) * GROUP for u in range(UNROLL_SHORT)]
        bases = [pl.multiple_of(f * heads, GROUP * heads) for f in firsts]
        pages = [[table[0, f + i] for i in range(GROUP)] for f in firsts]
        queries = [qs[pl.ds(b, GROUP * heads), :] for b in bases]
        scores = [dot_t(q.astype(BF16), joined(kp, p)) for q, p in zip(queries, pages)]
        valids = []
        for f in firsts:
            limit = jnp.full((1, GROUP * page), lens[0, f], jnp.int32)
            for i in range(1, GROUP):
                limit = jnp.where(lane_row >= i * page, lens[0, f + i], limit)
            valids.append(place < limit)
        finish(bases, queries, scores, valids, [lambda p=p: joined(vp, p) for p in pages])
        return carry

    lax.fori_loop(0, rows // (GROUP * UNROLL_SHORT), short_step, 0)

    span = lax.broadcasted_iota(jnp.int32, (heads, max_pages * page), 1)

    def long_step(step, carry):
        who = [longs[jnp.minimum(step * UNROLL_LONG + u, long_count - 1)] for u in range(UNROLL_LONG)]
        bases = [pl.multiple_of(r * heads, heads) for r in who]
        pages = [[table[j, r] for j in range(max_pages)] for r in who]
        queries = [qs[pl.ds(b, heads), :] for b in bases]
        scores = []
        for q, p in zip(queries, pages):
            q16 = q.astype(BF16)
            parts = [dot_t(q16, joined(kp, p[c : c + 4])) for c in range(0, max_pages, 4)]
            scores.append(jnp.concatenate(parts, axis=1))
        valids = [span < lens[0, r] for r in who]
        finish(bases, queries, scores, valids, [lambda p=p: joined(vp, p) for p in pages])
        return carry

    lax.fori_loop(0, (long_count + UNROLL_LONG - 1) // UNROLL_LONG, long_step, 0)

    for h in range(heads):
        att_out[:, h * head : (h + 1) * head] = os[pl.ds(h, rows, stride=heads), :].astype(BF16)
    for k in range(2):
        mig[k * 24 : k * 24 + 8, :] = os[pl.ds(pl.multiple_of(slots[k, req] * heads, heads), heads), :]
    mig_out[...] = mig[...].astype(BF16)
    for k in range(2):

        def depart(j, carry, k=k):
            held = table[j, slots[k, req]]
            at = pl.multiple_of(j * page, page)
            dk_out[k, pl.ds(at, page), :] = kp[held]
            dv_out[k, pl.ds(at, page), :] = vp[held]
            return carry

        lax.fori_loop(0, max_pages, depart, 0)


def attention(table, lens, slots, tokens, gain, wq, wk, wv, kc, vc):
    rows, _ = tokens.shape
    pool, _, page, head = kc.shape
    heads = wq.shape[1] // head
    span = table.shape[0] * page
    vmem = pl.BlockSpec(memory_space=pltpu.VMEM)
    hbm = pl.BlockSpec(memory_space=pltpu.HBM)
    return pl.pallas_call(
        attention_kernel,
        out_shape=(
            jax.ShapeDtypeStruct((rows, heads * head), BF16),
            jax.ShapeDtypeStruct((48, head), BF16),
            jax.ShapeDtypeStruct((2, span, head), BF16),
            jax.ShapeDtypeStruct((2, span, head), BF16),
        ),
        in_specs=[hbm] * 10,
        out_specs=(vmem,) * 4,
        scratch_shapes=[
            pltpu.SMEM(table.shape, jnp.int32),
            pltpu.SMEM((1, rows), jnp.int32),
            pltpu.VMEM((1, rows), jnp.int32),
            pltpu.SMEM(slots.shape, jnp.int32),
            pltpu.VMEM(tokens.shape, BF16),
            pltpu.VMEM(gain.shape, F32),
            pltpu.VMEM(wq.shape, BF16),
            pltpu.VMEM(wk.shape, BF16),
            pltpu.VMEM(wv.shape, BF16),
            pltpu.VMEM((pool, page, head), BF16),
            pltpu.VMEM((pool, page, head), BF16),
            pltpu.VMEM((rows * heads, head), F32),
            pltpu.VMEM((rows * heads, head), F32),
            pltpu.VMEM((rows * heads, head), F32),
            pltpu.VMEM((rows * heads, head), F32),
            pltpu.VMEM((48, head), F32),
            pltpu.SMEM((rows,), jnp.int32),
            pltpu.SemaphoreType.DMA((6,)),
            pltpu.SemaphoreType.DMA((QUERY_CUTS + 2,)),
            pltpu.SemaphoreType.DMA((2 * POOL_CUTS,)),
        ],
        compiler_params=pltpu.CompilerParams(vmem_limit_bytes=36 << 20),
        name="attention",
    )(*map(in_hbm, (table, lens, slots, tokens, gain, wq, wk, wv, kc, vc)))


def project_kernel(slots_hbm, attended, arrived, w_hbm, *rest):
    outs, (slots, w_out, partial, sem) = rest[:-4], rest[-4:]
    load = pltpu.make_async_copy(slots_hbm, slots, sem.at[0])
    load.start()
    cut = w_hbm.shape[1] // OUT_CUTS
    loads = []
    for c in range(OUT_CUTS):
        span = pl.ds(c * cut, cut)
        loads.append(pltpu.make_async_copy(w_hbm.at[:, span], w_out.at[:, span], sem.at[c + 1]))
        loads[-1].start()
    rows, _ = attended.shape
    block = rows // len(outs)
    head = arrived.shape[1]
    heads = attended.shape[1] // head
    row_id = lax.broadcasted_iota(jnp.int32, (rows, head), 0)
    got = arrived[...].astype(F32)
    req = lax.axis_index("req")
    kv = lax.axis_index("kv")
    load.wait()
    pieces = []
    for h in range(heads):
        piece = attended[:, h * head : (h + 1) * head].astype(F32)
        for k in range(2):
            piece = jnp.where(row_id == slots[k, req], got[k * 24 + h : k * 24 + h + 1, :], piece)
        pieces.append(piece.astype(BF16))
    settled = jnp.concatenate(pieces, axis=1)
    for c in range(OUT_CUTS):
        loads[c].wait()
        span = slice(c * cut, (c + 1) * cut)
        partial[:, span] = dot_n(settled, w_out[:, span]).astype(BF16)
    for s, out in enumerate(outs):
        at = lax.rem(kv + s, len(outs)) * block
        out[...] = partial[pl.ds(pl.multiple_of(at, block), block), :]


def project(slots, attended, arrived, w_out, count):
    vmem = pl.BlockSpec(memory_space=pltpu.VMEM)
    hbm = pl.BlockSpec(memory_space=pltpu.HBM)
    rows, width = attended.shape[0], w_out.shape[1]
    return pl.pallas_call(
        project_kernel,
        out_shape=[jax.ShapeDtypeStruct((rows // count, width), BF16)] * count,
        in_specs=[hbm, vmem, vmem, hbm],
        out_specs=[vmem] * count,
        scratch_shapes=[
            pltpu.SMEM(slots.shape, jnp.int32),
            pltpu.VMEM(w_out.shape, BF16),
            pltpu.VMEM((rows, width), BF16),
            pltpu.SemaphoreType.DMA((OUT_CUTS + 1,)),
        ],
        compiler_params=pltpu.CompilerParams(vmem_limit_bytes=16 << 20),
        name="project",
    )(in_hbm(slots), attended, arrived, in_hbm(w_out))


def scatter_kernel(
    slots_hbm,
    tokens_hbm,
    gain_hbm,
    own,
    one,
    two,
    three,
    arrived,
    hits,
    hidden,
    out,
    slots,
    tokens,
    gain,
    isem,
):
    rows, width = own.shape
    half = width // 2
    head = arrived.shape[1]
    req = lax.axis_index("req")
    at = lax.axis_index("kv") * rows
    loads = [
        pltpu.make_async_copy(slots_hbm, slots, isem.at[0]),
        pltpu.make_async_copy(
            tokens_hbm.at[pl.ds(pl.multiple_of(at, rows), rows)], tokens, isem.at[1]
        ),
        pltpu.make_async_copy(gain_hbm, gain, isem.at[2]),
    ]
    for load in loads:
        load.start()
    total = own[...].astype(F32)
    for other in (one, two, three):
        total = total + other[...].astype(F32)
    got = arrived[...].astype(F32)
    row_id = lax.broadcasted_iota(jnp.int32, (rows, 1), 0) + at
    for load in loads:
        load.wait()
    residual = tokens[...].astype(F32)
    for k in range(2):
        row = jnp.concatenate(
            [got[k * 24 + 8 + c : k * 24 + 9 + c, :] for c in range(width // head)], axis=1
        )
        residual = jnp.where(row_id == slots[k, req], row, residual)
    settled = (residual + total).astype(BF16)
    hidden[...] = settled
    x = settled.astype(F32)
    moe_in = (
        x * lax.rsqrt(jnp.mean(x * x, axis=-1, keepdims=True) + EPSILON) * gain[...]
    ).astype(BF16)
    stacked = jnp.concatenate([moe_in[:, :half], moe_in[:, half:]], axis=0)
    cut = 256
    for c in range(out.shape[0] // cut):
        span = pl.ds(c * cut, cut)
        out[span, :] = dot_n(hits[span, :], stacked).astype(BF16)


def scatter(slots, tokens, gain, blocks, arrived, hits):
    vmem = pl.BlockSpec(memory_space=pltpu.VMEM)
    hbm = pl.BlockSpec(memory_space=pltpu.HBM)
    rows, width = blocks[0].shape
    places = hits.shape[0]
    return pl.pallas_call(
        scatter_kernel,
        out_shape=(
            jax.ShapeDtypeStruct((rows, width), BF16),
            jax.ShapeDtypeStruct((places, width // 2), BF16),
        ),
        in_specs=[hbm] * 3 + [vmem] * 6,
        out_specs=(vmem, vmem),
        scratch_shapes=[
            pltpu.SMEM(slots.shape, jnp.int32),
            pltpu.VMEM((rows, width), BF16),
            pltpu.VMEM(gain.shape, F32),
            pltpu.SemaphoreType.DMA((3,)),
        ],
        compiler_params=pltpu.CompilerParams(vmem_limit_bytes=16 << 20),
        name="scatter",
    )(in_hbm(slots), in_hbm(tokens), in_hbm(gain), *blocks, arrived, hits)


def expert_kernel(received, wg, wu, wd, out, xs, made, osem):
    pairs = received.shape[0] // 16
    half = received.shape[1]
    cut = 256
    low = lax.broadcasted_iota(jnp.int32, (pairs, 8, cut), 1) < 4
    for c in range(half // cut):
        part = received[:, c * cut : (c + 1) * cut].astype(F32).reshape(pairs, 2, 8, cut)
        one, two = part[:, 0], part[:, 1]
        left = jnp.where(low, one, pltpu.roll(two, 4, 1))
        right = jnp.where(low, pltpu.roll(one, 4, 1), two)
        xs[:, c * cut : (c + 1) * cut] = left.reshape(pairs * 8, cut).astype(BF16)
        xs[:, half + c * cut : half + (c + 1) * cut] = right.reshape(pairs * 8, cut).astype(BF16)
    inputs = xs[...]
    gate = dot_n(inputs, wg[0])
    up = dot_n(inputs, wu[0])
    act = (gate / (1.0 + jnp.exp(-gate)) * up).astype(BF16)
    copies = []
    for c in range(half // cut):
        left = dot_n(act, wd[0, :, c * cut : (c + 1) * cut]).reshape(pairs, 8, cut)
        right = dot_n(act, wd[0, :, half + c * cut : half + (c + 1) * cut]).reshape(pairs, 8, cut)
        one = jnp.where(low, left, pltpu.roll(right, 4, 1))
        two = jnp.where(low, pltpu.roll(left, 4, 1), right)
        both = jnp.stack([one, two], axis=1).reshape(pairs * 16, cut)
        span = pl.ds(c * cut, cut)
        made[:, span] = both.astype(BF16)
        copies.append(pltpu.make_async_copy(made.at[:, span], out.at[:, span], osem.at[c]))
        copies[-1].start()
    for copy in copies:
        copy.wait()


def expert(received, wg, wu, wd):
    vmem = pl.BlockSpec(memory_space=pltpu.VMEM)
    rows, half = received.shape
    return pl.pallas_call(
        expert_kernel,
        out_shape=jax.ShapeDtypeStruct((rows, half), BF16),
        in_specs=[vmem] * 4,
        out_specs=pl.BlockSpec(memory_space=pltpu.HBM),
        scratch_shapes=[
            pltpu.VMEM((rows // 2, 2 * half), BF16),
            pltpu.VMEM((rows, half), BF16),
            pltpu.SemaphoreType.DMA((half // 256,)),
        ],
        compiler_params=pltpu.CompilerParams(vmem_limit_bytes=40 << 20),
        name="expert",
    )(received, wg, wu, wd)


def settle_kernel(
    lens_hbm,
    slots_hbm,
    keys,
    values,
    keys_out,
    values_out,
    lens,
    slots,
    sem,
):
    reqs = lens_hbm.shape[0]
    partner = lax.rem(lax.axis_index("req") + reqs // 2, reqs)
    first = pltpu.make_async_copy(lens_hbm.at[pl.ds(partner, 1)], lens, sem.at[0])
    second = pltpu.make_async_copy(slots_hbm, slots, sem.at[1])
    first.start()
    second.start()
    first.wait()
    second.wait()
    cut = 256
    at = lax.broadcasted_iota(jnp.int32, (cut, keys.shape[2]), 0)
    for k in range(2):
        length = lens[0, slots[k, partner]]
        for c in range(keys.shape[1] // cut):
            keep = at < length - c * cut
            span = slice(c * cut, (c + 1) * cut)
            for src, dst in ((keys, keys_out), (values, values_out)):
                dst[k, span, :] = jnp.where(keep, src[k, span, :].astype(F32), 0.0).astype(BF16)


def settle(lens, slots, keys, values):
    vmem = pl.BlockSpec(memory_space=pltpu.VMEM)
    hbm = pl.BlockSpec(memory_space=pltpu.HBM)
    return pl.pallas_call(
        settle_kernel,
        out_shape=(
            jax.ShapeDtypeStruct(keys.shape, BF16),
            jax.ShapeDtypeStruct(values.shape, BF16),
        ),
        in_specs=[hbm] * 2 + [vmem] * 2,
        out_specs=(vmem,) * 2,
        scratch_shapes=[
            pltpu.SMEM((1, lens.shape[1]), jnp.int32),
            pltpu.SMEM(slots.shape, jnp.int32),
            pltpu.SemaphoreType.DMA((2,)),
        ],
        compiler_params=pltpu.CompilerParams(vmem_limit_bytes=20 << 20),
        name="settle",
    )(in_hbm(lens), in_hbm(slots), keys, values)


def body(
    tokens,
    lengths,
    page_table,
    key_cache,
    value_page_cache,
    mig_slot,
    attn_gain,
    w_query,
    key_weight,
    value_weight,
    w_out,
    moe_gain,
    routes,
    gate_probs,
    w_gate,
    w_up,
    w_down,
):
    req_count = lax.axis_size("req")
    kv_count = lax.axis_size("kv")
    requests_here, _ = tokens.shape
    table = page_table.T
    mig_rows = mig_slot.T
    length_rows = lengths.reshape(req_count, requests_here)
    swap = [(i, (i + req_count // 2) % req_count) for i in range(req_count)]
    attended, leaving, depart_keys, depart_values = attention(
        table,
        length_rows,
        mig_rows,
        tokens,
        attn_gain[None, :],
        w_query,
        key_weight,
        value_weight,
        key_cache,
        value_page_cache,
    )
    arrived = lax.ppermute(leaving, "req", swap)
    arrived_keys = lax.ppermute(depart_keys, "req", swap)
    arrived_values = lax.ppermute(depart_values, "req", swap)
    disp_rows = requests_here // kv_count
    blocks = list(project(mig_rows, attended, arrived, w_out, kv_count))
    for s in range(1, kv_count):
        blocks[s] = lax.ppermute(blocks[s], "kv", [(i, (i + s) % kv_count) for i in range(kv_count)])

    devices = req_count * kv_count
    top_count = routes.shape[1]
    capacity = 2 * disp_rows * top_count // devices
    flat_routes = routes.reshape(-1)
    ids = jnp.arange(disp_rows * top_count, dtype=jnp.int32)
    earlier = (flat_routes[:, None] == flat_routes[None, :]) & (ids[None, :] < ids[:, None])
    ranking = jnp.sum(earlier.astype(jnp.int32), axis=1)
    slot_index = (flat_routes * capacity + ranking).reshape(disp_rows, top_count)
    chunk_rows = 2 * capacity
    places = jnp.arange(devices * chunk_rows, dtype=jnp.int32)
    place_slot = (places // chunk_rows) * capacity + places % capacity
    place_half = (places % chunk_rows) // capacity
    stacked_slots = jnp.concatenate([slot_index, slot_index], axis=0)
    row_half = jnp.arange(2 * disp_rows, dtype=jnp.int32) // disp_rows
    hits = jnp.any(place_slot[:, None, None] == stacked_slots.T[None, :, :], axis=1)
    hits = (hits & (place_half[:, None] == row_half[None, :])).astype(BF16)
    hidden, outgoing = scatter(mig_rows, tokens, moe_gain[None, :], blocks, arrived, hits)

    shares = gate_probs / jnp.sum(gate_probs, axis=1, keepdims=True)
    stacked_shares = jnp.concatenate([shares, shares], axis=0)
    share_map = jnp.sum(
        jnp.where(
            (place_slot[None, None, :] == stacked_slots[:, :, None])
            & (place_half[None, None, :] == row_half[:, None, None]),
            stacked_shares[:, :, None],
            0.0,
        ),
        axis=1,
    )
    share_high = share_map.astype(BF16)
    share_low = (share_map - share_high.astype(F32)).astype(BF16)
    share_rows = jnp.concatenate([share_high, share_low], axis=0)

    arrived_keys, arrived_values = settle(length_rows, mig_rows, arrived_keys, arrived_values)
    received = lax.all_to_all(outgoing, ("req", "kv"), split_axis=0, concat_axis=0, tiled=True)
    made = expert(received, w_gate, w_up, w_down)
    returned = lax.all_to_all(made, ("req", "kv"), split_axis=0, concat_axis=0, tiled=True)
    mixed = dot_n(share_rows, returned)
    mixed = mixed[: 2 * disp_rows] + mixed[2 * disp_rows :]
    mixed = jnp.concatenate([mixed[:disp_rows], mixed[disp_rows:]], axis=1)
    layer_out = (hidden.astype(F32) + mixed).astype(BF16)
    return (layer_out, arrived_keys[:, None], arrived_values[:, None])


def solution(mesh):
    in_specs = (
        P("req", None),
        P(),
        P("req", None),
        P("req", "kv", None, None),
        P("req", "kv", None, None),
        P(),
        P(),
        P(None, "kv"),
        P(None, "kv"),
        P(None, "kv"),
        P("kv", None),
        P(),
        P(("req", "kv"), None),
        P(("req", "kv"), None),
        P(("req", "kv"), None, None),
        P(("req", "kv"), None, None),
        P(("req", "kv"), None, None),
    )
    out_specs = (P(("req", "kv"), None), P("req", "kv", None, None), P("req", "kv", None, None))

    return jax.shard_map(body, mesh=mesh, in_specs=in_specs, out_specs=out_specs, check_vma=False)
```

```python
import math

import jax
import jax.numpy as jnp
from jax import lax
from jax.experimental import pallas as pl
from jax.experimental.pallas import tpu as pltpu
from jax.sharding import PartitionSpec as P

EPSILON = 1e-06
THETA = 1000000.0
MASKED = -1e30
BF16 = jnp.bfloat16
F32 = jnp.float32
POOL_CUTS = 1
QUERY_CUTS = 2
OUT_CUTS = 2
MIX_CUTS = 2
GROUP = 4
UNROLL_SHORT = 16
UNROLL_LONG = 8


def dot_t(a, b):
    return lax.dot_general(a, b, (((1,), (1,)), ((), ())), preferred_element_type=F32)


def dot_n(a, b):
    return jnp.dot(a, b, preferred_element_type=F32)


def in_hbm(x):
    return pltpu.with_memory_space_constraint(x, pltpu.HBM)


def attention_kernel(
    table_hbm,
    lens_hbm,
    slots_hbm,
    tokens_hbm,
    gain_hbm,
    wq_hbm,
    wk_hbm,
    wv_hbm,
    k_hbm,
    v_hbm,
    att_out,
    mig_out,
    caches_out,
    table,
    lens,
    lens_row,
    slots,
    tokens,
    gain,
    wq,
    wk,
    wv,
    kp,
    vp,
    qs,
    ks,
    vs,
    os,
    mig,
    longs,
    isem,
    wsem,
    psem,
):
    rows, width = tokens.shape
    pool, page, head = kp.shape
    max_pages = table.shape[0]
    heads = wq.shape[1] // head
    scale = 1.0 / math.sqrt(head)
    wcut = wq.shape[1] // QUERY_CUTS
    pcut = pool // POOL_CUTS
    req = lax.axis_index("req")

    icopies = [
        pltpu.make_async_copy(tokens_hbm, tokens, isem.at[0]),
        pltpu.make_async_copy(gain_hbm, gain, isem.at[1]),
        pltpu.make_async_copy(lens_hbm.at[pl.ds(req, 1)], lens_row, isem.at[2]),
        pltpu.make_async_copy(lens_hbm.at[pl.ds(req, 1)], lens, isem.at[3]),
        pltpu.make_async_copy(table_hbm, table, isem.at[4]),
        pltpu.make_async_copy(slots_hbm, slots, isem.at[5]),
    ]
    wcopies = [
        pltpu.make_async_copy(
            wq_hbm.at[:, pl.ds(c * wcut, wcut)], wq.at[:, pl.ds(c * wcut, wcut)], wsem.at[c]
        )
        for c in range(QUERY_CUTS)
    ]
    wcopies.append(pltpu.make_async_copy(wk_hbm, wk, wsem.at[QUERY_CUTS]))
    wcopies.append(pltpu.make_async_copy(wv_hbm, wv, wsem.at[QUERY_CUTS + 1]))
    pcopies = []
    for i, (src, dst) in enumerate(((k_hbm, kp), (v_hbm, vp))):
        for c in range(POOL_CUTS):
            pcopies.append(
                pltpu.make_async_copy(
                    src.at[pl.ds(c * pcut, pcut), 0],
                    dst.at[pl.ds(c * pcut, pcut)],
                    psem.at[i * POOL_CUTS + c],
                )
            )
    for copy in icopies + wcopies + pcopies:
        copy.start()
    for copy in icopies:
        copy.wait()

    def gather_long(r, n):
        is_long = lens[0, r] > page

        @pl.when(is_long)
        def _():
            longs[n] = r

        return n + is_long.astype(jnp.int32)

    long_count = lax.fori_loop(0, rows, gather_long, jnp.int32(0))

    positions = jnp.broadcast_to(lens_row[...], (rows, rows)).astype(F32).T
    half_lane = lax.broadcasted_iota(jnp.int32, (1, head), 1)
    exponent = (half_lane % (head // 2)).astype(F32) * (-2.0 / head)
    angles = positions * jnp.exp(exponent * math.log(THETA))
    cos = jnp.cos(angles)
    sin = jnp.where(half_lane < head // 2, -1.0, 1.0) * jnp.sin(angles)

    x = tokens[...].astype(F32)
    row_id = lax.broadcasted_iota(jnp.int32, (rows, 1), 0)
    for k in range(2):
        leaving = jnp.sum(jnp.where(row_id == slots[k, req], x, 0.0), axis=0, keepdims=True)
        for c in range(width // head):
            mig[k * 24 + 8 + c : k * 24 + 9 + c, :] = leaving[:, c * head : (c + 1) * head]
    normed = (
        x * lax.rsqrt(jnp.mean(x * x, axis=-1, keepdims=True) + EPSILON) * gain[...]
    ).astype(BF16)

    def rotated(vectors):
        unit = vectors * lax.rsqrt(jnp.mean(vectors * vectors, axis=-1, keepdims=True) + EPSILON)
        turned = unit * cos + pltpu.roll(unit, head // 2, 1) * sin
        return turned.astype(BF16).astype(F32)

    per_cut = wcut // head
    for c in range(QUERY_CUTS):
        wcopies[c].wait()
        query = dot_n(normed, wq[:, c * wcut : (c + 1) * wcut])
        for i in range(per_cut):
            qs[pl.ds(c * per_cut + i, rows, stride=heads), :] = rotated(
                query[:, i * head : (i + 1) * head]
            )
    wcopies[QUERY_CUTS].wait()
    wcopies[QUERY_CUTS + 1].wait()
    fresh_key = rotated(dot_n(normed, wk[...]))
    fresh_value = dot_n(normed, wv[...]).astype(BF16).astype(F32)
    for h in range(heads):
        ks[pl.ds(h, rows, stride=heads), :] = fresh_key
        vs[pl.ds(h, rows, stride=heads), :] = fresh_value

    for copy in pcopies:
        copy.wait()

    def finish(bases, queries, scores, valids, values):
        count = queries[0].shape[0]
        scores = [jnp.where(v, x * scale, MASKED) for v, x in zip(valids, scores)]
        selves = [
            jnp.sum(q * ks[pl.ds(b, count), :], axis=1, keepdims=True) * scale
            for b, q in zip(bases, queries)
        ]
        tops = [
            jnp.maximum(jnp.max(x, axis=1, keepdims=True), y) for x, y in zip(scores, selves)
        ]
        weights = [jnp.exp(x - t) for x, t in zip(scores, tops)]
        summed = [dot_n(w.astype(BF16), v()) for w, v in zip(weights, values)]
        selves = [jnp.exp(y - t) for y, t in zip(selves, tops)]
        totals = [jnp.sum(w, axis=1, keepdims=True) + y for w, y in zip(weights, selves)]
        for b, y, t, o in zip(bases, selves, totals, summed):
            fresh = y.astype(BF16).astype(F32) * vs[pl.ds(b, count), :]
            os[pl.ds(b, count), :] = (o + fresh) / t

    lanes = lax.broadcasted_iota(jnp.int32, (GROUP * heads, GROUP * page), 1)
    subs = lax.broadcasted_iota(jnp.int32, (GROUP * heads, GROUP * page), 0)
    place = jnp.where(lanes // page == subs // heads, lanes % page, 1 << 20)
    lane_row = lax.broadcasted_iota(jnp.int32, (1, GROUP * page), 1)

    def joined(pool_ref, pages):
        return jnp.concatenate([pool_ref[p] for p in pages], axis=0)

    def short_step(step, carry):
        firsts = [(step * UNROLL_SHORT + u) * GROUP for u in range(UNROLL_SHORT)]
        bases = [pl.multiple_of(f * heads, GROUP * heads) for f in firsts]
        pages = [[table[0, f + i] for i in range(GROUP)] for f in firsts]
        queries = [qs[pl.ds(b, GROUP * heads), :] for b in bases]
        scores = [dot_t(q.astype(BF16), joined(kp, p)) for q, p in zip(queries, pages)]
        valids = []
        for f in firsts:
            limit = jnp.full((1, GROUP * page), lens[0, f], jnp.int32)
            for i in range(1, GROUP):
                limit = jnp.where(lane_row >= i * page, lens[0, f + i], limit)
            valids.append(place < limit)
        finish(bases, queries, scores, valids, [lambda p=p: joined(vp, p) for p in pages])
        return carry

    lax.fori_loop(0, rows // (GROUP * UNROLL_SHORT), short_step, 0)

    span = lax.broadcasted_iota(jnp.int32, (heads, max_pages * page), 1)

    def long_step(step, carry):
        who = [longs[jnp.minimum(step * UNROLL_LONG + u, long_count - 1)] for u in range(UNROLL_LONG)]
        bases = [pl.multiple_of(r * heads, heads) for r in who]
        pages = [[table[j, r] for j in range(max_pages)] for r in who]
        queries = [qs[pl.ds(b, heads), :] for b in bases]
        scores = []
        for q, p in zip(queries, pages):
            q16 = q.astype(BF16)
            parts = [dot_t(q16, joined(kp, p[c : c + 4])) for c in range(0, max_pages, 4)]
            scores.append(jnp.concatenate(parts, axis=1))
        valids = [span < lens[0, r] for r in who]
        finish(bases, queries, scores, valids, [lambda p=p: joined(vp, p) for p in pages])
        return carry

    lax.fori_loop(0, (long_count + UNROLL_LONG - 1) // UNROLL_LONG, long_step, 0)

    for h in range(heads):
        att_out[:, h * head : (h + 1) * head] = os[pl.ds(h, rows, stride=heads), :].astype(BF16)
    for k in range(2):
        mig[k * 24 : k * 24 + 8, :] = os[pl.ds(pl.multiple_of(slots[k, req] * heads, heads), heads), :]
    mig_out[...] = mig[...].astype(BF16)
    for k in range(2):

        def depart(j, carry, k=k):
            held = table[j, slots[k, req]]
            at = pl.multiple_of(j * page, page)
            caches_out[k, pl.ds(at, page), :] = kp[held]
            caches_out[2 + k, pl.ds(at, page), :] = vp[held]
            return carry

        lax.fori_loop(0, max_pages, depart, 0, unroll=4)


def attention(table, lens, slots, tokens, gain, wq, wk, wv, kc, vc):
    rows, _ = tokens.shape
    pool, _, page, head = kc.shape
    heads = wq.shape[1] // head
    span = table.shape[0] * page
    vmem = pl.BlockSpec(memory_space=pltpu.VMEM)
    hbm = pl.BlockSpec(memory_space=pltpu.HBM)
    return pl.pallas_call(
        attention_kernel,
        out_shape=(
            jax.ShapeDtypeStruct((rows, heads * head), BF16),
            jax.ShapeDtypeStruct((48, head), BF16),
            jax.ShapeDtypeStruct((4, span, head), BF16),
        ),
        in_specs=[hbm] * 10,
        out_specs=(vmem,) * 3,
        scratch_shapes=[
            pltpu.SMEM(table.shape, jnp.int32),
            pltpu.SMEM((1, rows), jnp.int32),
            pltpu.VMEM((1, rows), jnp.int32),
            pltpu.SMEM(slots.shape, jnp.int32),
            pltpu.VMEM(tokens.shape, BF16),
            pltpu.VMEM(gain.shape, F32),
            pltpu.VMEM(wq.shape, BF16),
            pltpu.VMEM(wk.shape, BF16),
            pltpu.VMEM(wv.shape, BF16),
            pltpu.VMEM((pool, page, head), BF16),
            pltpu.VMEM((pool, page, head), BF16),
            pltpu.VMEM((rows * heads, head), F32),
            pltpu.VMEM((rows * heads, head), F32),
            pltpu.VMEM((rows * heads, head), F32),
            pltpu.VMEM((rows * heads, head), F32),
            pltpu.VMEM((48, head), F32),
            pltpu.SMEM((rows,), jnp.int32),
            pltpu.SemaphoreType.DMA((6,)),
            pltpu.SemaphoreType.DMA((QUERY_CUTS + 2,)),
            pltpu.SemaphoreType.DMA((2 * POOL_CUTS,)),
        ],
        compiler_params=pltpu.CompilerParams(vmem_limit_bytes=36 << 20),
        name="attention",
    )(*map(in_hbm, (table, lens, slots, tokens, gain, wq, wk, wv, kc, vc)))


def project_kernel(slots_hbm, attended, arrived, w_hbm, *rest):
    outs, (slots, w_out, partial, sem) = rest[:-4], rest[-4:]
    load = pltpu.make_async_copy(slots_hbm, slots, sem.at[0])
    load.start()
    cut = w_hbm.shape[1] // OUT_CUTS
    loads = []
    for c in range(OUT_CUTS):
        span = pl.ds(c * cut, cut)
        loads.append(pltpu.make_async_copy(w_hbm.at[:, span], w_out.at[:, span], sem.at[c + 1]))
        loads[-1].start()
    rows, _ = attended.shape
    block = rows // len(outs)
    head = arrived.shape[1]
    heads = attended.shape[1] // head
    row_id = lax.broadcasted_iota(jnp.int32, (rows, head), 0)
    got = arrived[...].astype(F32)
    req = lax.axis_index("req")
    kv = lax.axis_index("kv")
    load.wait()
    pieces = []
    for h in range(heads):
        piece = attended[:, h * head : (h + 1) * head].astype(F32)
        for k in range(2):
            piece = jnp.where(row_id == slots[k, req], got[k * 24 + h : k * 24 + h + 1, :], piece)
        pieces.append(piece.astype(BF16))
    settled = jnp.concatenate(pieces, axis=1)
    for c in range(OUT_CUTS):
        loads[c].wait()
        span = slice(c * cut, (c + 1) * cut)
        partial[:, span] = dot_n(settled, w_out[:, span]).astype(BF16)
    for s, out in enumerate(outs):
        at = lax.rem(kv + s, len(outs)) * block
        out[...] = partial[pl.ds(pl.multiple_of(at, block), block), :]


def project(slots, attended, arrived, w_out, count):
    vmem = pl.BlockSpec(memory_space=pltpu.VMEM)
    hbm = pl.BlockSpec(memory_space=pltpu.HBM)
    rows, width = attended.shape[0], w_out.shape[1]
    return pl.pallas_call(
        project_kernel,
        out_shape=[jax.ShapeDtypeStruct((rows // count, width), BF16)] * count,
        in_specs=[hbm, vmem, vmem, hbm],
        out_specs=[vmem] * count,
        scratch_shapes=[
            pltpu.SMEM(slots.shape, jnp.int32),
            pltpu.VMEM(w_out.shape, BF16),
            pltpu.VMEM((rows, width), BF16),
            pltpu.SemaphoreType.DMA((OUT_CUTS + 1,)),
        ],
        compiler_params=pltpu.CompilerParams(vmem_limit_bytes=16 << 20),
        name="project",
    )(in_hbm(slots), attended, arrived, in_hbm(w_out))


def scatter_kernel(
    slots_hbm,
    tokens_hbm,
    gain_hbm,
    own,
    one,
    two,
    three,
    arrived,
    hits,
    hidden,
    out,
    slots,
    tokens,
    gain,
    isem,
):
    rows, width = own.shape
    half = width // 2
    head = arrived.shape[1]
    req = lax.axis_index("req")
    at = lax.axis_index("kv") * rows
    loads = [
        pltpu.make_async_copy(slots_hbm, slots, isem.at[0]),
        pltpu.make_async_copy(
            tokens_hbm.at[pl.ds(pl.multiple_of(at, rows), rows)], tokens, isem.at[1]
        ),
        pltpu.make_async_copy(gain_hbm, gain, isem.at[2]),
    ]
    for load in loads:
        load.start()
    total = own[...].astype(F32)
    for other in (one, two, three):
        total = total + other[...].astype(F32)
    got = arrived[...].astype(F32)
    row_id = lax.broadcasted_iota(jnp.int32, (rows, 1), 0) + at
    for load in loads:
        load.wait()
    residual = tokens[...].astype(F32)
    for k in range(2):
        row = jnp.concatenate(
            [got[k * 24 + 8 + c : k * 24 + 9 + c, :] for c in range(width // head)], axis=1
        )
        residual = jnp.where(row_id == slots[k, req], row, residual)
    settled = (residual + total).astype(BF16)
    hidden[...] = settled
    x = settled.astype(F32)
    moe_in = (
        x * lax.rsqrt(jnp.mean(x * x, axis=-1, keepdims=True) + EPSILON) * gain[...]
    ).astype(BF16)
    stacked = jnp.concatenate([moe_in[:, :half], moe_in[:, half:]], axis=0)
    cut = 256
    for c in range(out.shape[0] // cut):
        span = pl.ds(c * cut, cut)
        out[span, :] = dot_n(hits[span, :], stacked).astype(BF16)


def scatter(slots, tokens, gain, blocks, arrived, hits):
    vmem = pl.BlockSpec(memory_space=pltpu.VMEM)
    hbm = pl.BlockSpec(memory_space=pltpu.HBM)
    rows, width = blocks[0].shape
    places = hits.shape[0]
    return pl.pallas_call(
        scatter_kernel,
        out_shape=(
            jax.ShapeDtypeStruct((rows, width), BF16),
            jax.ShapeDtypeStruct((places, width // 2), BF16),
        ),
        in_specs=[hbm] * 3 + [vmem] * 6,
        out_specs=(vmem, vmem),
        scratch_shapes=[
            pltpu.SMEM(slots.shape, jnp.int32),
            pltpu.VMEM((rows, width), BF16),
            pltpu.VMEM(gain.shape, F32),
            pltpu.SemaphoreType.DMA((3,)),
        ],
        compiler_params=pltpu.CompilerParams(vmem_limit_bytes=16 << 20),
        name="scatter",
    )(in_hbm(slots), in_hbm(tokens), in_hbm(gain), *blocks, arrived, hits)


def expert_kernel(received, wg, wu, wd, out, xs, made, osem):
    pairs = received.shape[0] // 16
    half = received.shape[1]
    cut = 256
    low = lax.broadcasted_iota(jnp.int32, (pairs, 8, cut), 1) < 4
    for c in range(half // cut):
        part = received[:, c * cut : (c + 1) * cut].astype(F32).reshape(pairs, 2, 8, cut)
        one, two = part[:, 0], part[:, 1]
        left = jnp.where(low, one, pltpu.roll(two, 4, 1))
        right = jnp.where(low, pltpu.roll(one, 4, 1), two)
        xs[:, c * cut : (c + 1) * cut] = left.reshape(pairs * 8, cut).astype(BF16)
        xs[:, half + c * cut : half + (c + 1) * cut] = right.reshape(pairs * 8, cut).astype(BF16)
    inputs = xs[...]
    gate = dot_n(inputs, wg[0])
    up = dot_n(inputs, wu[0])
    act = (gate / (1.0 + jnp.exp(-gate)) * up).astype(BF16)
    copies = []
    for c in range(half // cut):
        left = dot_n(act, wd[0, :, c * cut : (c + 1) * cut]).reshape(pairs, 8, cut)
        right = dot_n(act, wd[0, :, half + c * cut : half + (c + 1) * cut]).reshape(pairs, 8, cut)
        one = jnp.where(low, left, pltpu.roll(right, 4, 1))
        two = jnp.where(low, pltpu.roll(left, 4, 1), right)
        both = jnp.stack([one, two], axis=1).reshape(pairs * 16, cut)
        span = pl.ds(c * cut, cut)
        made[:, span] = both.astype(BF16)
        copies.append(pltpu.make_async_copy(made.at[:, span], out.at[:, span], osem.at[c]))
        copies[-1].start()
    for copy in copies:
        copy.wait()


def expert(received, wg, wu, wd):
    vmem = pl.BlockSpec(memory_space=pltpu.VMEM)
    rows, half = received.shape
    return pl.pallas_call(
        expert_kernel,
        out_shape=jax.ShapeDtypeStruct((rows, half), BF16),
        in_specs=[vmem] * 4,
        out_specs=pl.BlockSpec(memory_space=pltpu.HBM),
        scratch_shapes=[
            pltpu.VMEM((rows // 2, 2 * half), BF16),
            pltpu.VMEM((rows, half), BF16),
            pltpu.SemaphoreType.DMA((half // 256,)),
        ],
        compiler_params=pltpu.CompilerParams(vmem_limit_bytes=40 << 20),
        name="expert",
    )(received, wg, wu, wd)


def settle_kernel(
    lens_hbm,
    slots_hbm,
    caches,
    keys_out,
    values_out,
    lens,
    slots,
    sem,
):
    reqs = lens_hbm.shape[0]
    partner = lax.rem(lax.axis_index("req") + reqs // 2, reqs)
    first = pltpu.make_async_copy(lens_hbm.at[pl.ds(partner, 1)], lens, sem.at[0])
    second = pltpu.make_async_copy(slots_hbm, slots, sem.at[1])
    first.start()
    second.start()
    first.wait()
    second.wait()
    cut = 256
    at = lax.broadcasted_iota(jnp.int32, (cut, caches.shape[2]), 0)
    for k in range(2):
        length = lens[0, slots[k, partner]]
        for c in range(caches.shape[1] // cut):
            keep = at < length - c * cut
            span = slice(c * cut, (c + 1) * cut)
            for i, dst in enumerate((keys_out, values_out)):
                held = caches[2 * i + k, span, :].astype(F32)
                dst[k, span, :] = jnp.where(keep, held, 0.0).astype(BF16)


def settle(lens, slots, caches):
    vmem = pl.BlockSpec(memory_space=pltpu.VMEM)
    hbm = pl.BlockSpec(memory_space=pltpu.HBM)
    return pl.pallas_call(
        settle_kernel,
        out_shape=(
            jax.ShapeDtypeStruct((2,) + caches.shape[1:], BF16),
            jax.ShapeDtypeStruct((2,) + caches.shape[1:], BF16),
        ),
        in_specs=[hbm] * 2 + [vmem],
        out_specs=(vmem,) * 2,
        scratch_shapes=[
            pltpu.SMEM((1, lens.shape[1]), jnp.int32),
            pltpu.SMEM(slots.shape, jnp.int32),
            pltpu.SemaphoreType.DMA((2,)),
        ],
        compiler_params=pltpu.CompilerParams(vmem_limit_bytes=4 << 20),
        name="settle",
    )(in_hbm(lens), in_hbm(slots), caches)


def combine_kernel(ret_hbm, high, low, hidden, out, ret, sem):
    rows, width = hidden.shape
    half = width // 2
    cut = ret.shape[0] // MIX_CUTS
    loads = []
    for c in range(MIX_CUTS):
        span = pl.ds(c * cut, cut)
        loads.append(pltpu.make_async_copy(ret_hbm.at[span], ret.at[span], sem.at[c]))
        loads[-1].start()
    shares = jnp.concatenate([high[...], low[...]], axis=0)
    mixed = jnp.zeros((4 * rows, half), F32)
    for c in range(MIX_CUTS):
        loads[c].wait()
        span = slice(c * cut, (c + 1) * cut)
        mixed = mixed + dot_n(shares[:, span], ret[span, :])
    mixed = mixed[: 2 * rows] + mixed[2 * rows :]
    kept = hidden[...].astype(F32)
    out[:, :half] = (kept[:, :half] + mixed[:rows]).astype(BF16)
    out[:, half:] = (kept[:, half:] + mixed[rows:]).astype(BF16)


def combine(returned, high, low, hidden):
    vmem = pl.BlockSpec(memory_space=pltpu.VMEM)
    return pl.pallas_call(
        combine_kernel,
        out_shape=jax.ShapeDtypeStruct(hidden.shape, BF16),
        in_specs=[pl.BlockSpec(memory_space=pltpu.HBM)] + [vmem] * 3,
        out_specs=vmem,
        scratch_shapes=[
            pltpu.VMEM(returned.shape, BF16),
            pltpu.SemaphoreType.DMA((MIX_CUTS,)),
        ],
        compiler_params=pltpu.CompilerParams(vmem_limit_bytes=12 << 20),
        name="combine",
    )(in_hbm(returned), high, low, hidden)


def body(
    tokens,
    lengths,
    page_table,
    key_cache,
    value_page_cache,
    mig_slot,
    attn_gain,
    w_query,
    key_weight,
    value_weight,
    w_out,
    moe_gain,
    routes,
    gate_probs,
    w_gate,
    w_up,
    w_down,
):
    req_count = lax.axis_size("req")
    kv_count = lax.axis_size("kv")
    requests_here, _ = tokens.shape
    table = page_table.T
    mig_rows = mig_slot.T
    length_rows = lengths.reshape(req_count, requests_here)
    swap = [(i, (i + req_count // 2) % req_count) for i in range(req_count)]
    attended, leaving, caches = attention(
        table,
        length_rows,
        mig_rows,
        tokens,
        attn_gain[None, :],
        w_query,
        key_weight,
        value_weight,
        key_cache,
        value_page_cache,
    )
    arrived = lax.ppermute(leaving, "req", swap)
    caches = lax.ppermute(caches, "req", swap)
    disp_rows = requests_here // kv_count
    blocks = list(project(mig_rows, attended, arrived, w_out, kv_count))
    for s in range(1, kv_count):
        blocks[s] = lax.ppermute(blocks[s], "kv", [(i, (i + s) % kv_count) for i in range(kv_count)])

    devices = req_count * kv_count
    top_count = routes.shape[1]
    capacity = 2 * disp_rows * top_count // devices
    flat_routes = routes.reshape(-1)
    ids = jnp.arange(disp_rows * top_count, dtype=jnp.int32)
    earlier = (flat_routes[:, None] == flat_routes[None, :]) & (ids[None, :] < ids[:, None])
    ranking = jnp.sum(earlier.astype(jnp.int32), axis=1)
    slot_index = (flat_routes * capacity + ranking).reshape(disp_rows, top_count)
    chunk_rows = 2 * capacity
    places = jnp.arange(devices * chunk_rows, dtype=jnp.int32)
    place_slot = (places // chunk_rows) * capacity + places % capacity
    place_half = (places % chunk_rows) // capacity
    stacked_slots = jnp.concatenate([slot_index, slot_index], axis=0)
    row_half = jnp.arange(2 * disp_rows, dtype=jnp.int32) // disp_rows
    hits = jnp.any(place_slot[:, None, None] == stacked_slots.T[None, :, :], axis=1)
    hits = (hits & (place_half[:, None] == row_half[None, :])).astype(BF16)
    hidden, outgoing = scatter(mig_rows, tokens, moe_gain[None, :], blocks, arrived, hits)

    shares = gate_probs / jnp.sum(gate_probs, axis=1, keepdims=True)
    stacked_shares = jnp.concatenate([shares, shares], axis=0)
    share_map = jnp.sum(
        jnp.where(
            (place_slot[None, None, :] == stacked_slots[:, :, None])
            & (place_half[None, None, :] == row_half[:, None, None]),
            stacked_shares[:, :, None],
            0.0,
        ),
        axis=1,
    )
    share_high = share_map.astype(BF16)
    share_low = (share_map - share_high.astype(F32)).astype(BF16)

    arrived_keys, arrived_values = settle(length_rows, mig_rows, caches)
    received = lax.all_to_all(outgoing, ("req", "kv"), split_axis=0, concat_axis=0, tiled=True)
    made = expert(received, w_gate, w_up, w_down)
    returned = lax.all_to_all(made, ("req", "kv"), split_axis=0, concat_axis=0, tiled=True)
    layer_out = combine(returned, share_high, share_low, hidden)
    return (layer_out, arrived_keys[:, None], arrived_values[:, None])


def solution(mesh):
    in_specs = (
        P("req", None),
        P(),
        P("req", None),
        P("req", "kv", None, None),
        P("req", "kv", None, None),
        P(),
        P(),
        P(None, "kv"),
        P(None, "kv"),
        P(None, "kv"),
        P("kv", None),
        P(),
        P(("req", "kv"), None),
        P(("req", "kv"), None),
        P(("req", "kv"), None, None),
        P(("req", "kv"), None, None),
        P(("req", "kv"), None, None),
    )
    out_specs = (P(("req", "kv"), None), P("req", "kv", None, None), P("req", "kv", None, None))

    return jax.shard_map(body, mesh=mesh, in_specs=in_specs, out_specs=out_specs, check_vma=False)
```
